32 devices in a mesh: depth: 4 (over z), lat: 8 (over y, x, core).
Axes of the slice: x: 2, y: 2, z: 4, core: 2. Of those that a mesh axis runs over, the one named last changes fastest.
Arguments:
- volume_init: float32 [16, 64, 16, 128], P('depth', 'lat'), may hold values from 0.2 to 10
- measured: float32 [64, 16, 128], P('lat'), may hold values from 0.25 to 4
- psf: bfloat16 [16, 13, 128, 128], P('depth'), may hold values from 0 to 0.0043269231
- offsets: int32 [16, 13], replicated, may hold values from 0 to 24, as said below
- counts: int32 [16], replicated, may hold values from 1 to 13, 130 in all
Outputs:
- volume: float32 [16, 64, 16, 128], P('depth', 'lat')
The draws below stay inside these ranges and needn't reach their ends.
Inputs may be any that keep to these rules, and one draw needn't show every extreme that they name: `offsets`: entry v names the block offset (v // 5 - 2, v % 5 - 2) in patch rows and patches; the entries of one depth are distinct, and entry 0 of every depth is the central offset 2 * 5 + 2.
All inputs are finite; a program needn't handle non-finite values.
Results may differ from the reference program's by a relative error of at most 0.00076.
Values may be sent and summed in bfloat16 or wider, within the bound.
A program may use at most 64 MiB of HBM per device.

```python
import math
import jax
import jax.numpy as jnp
import numpy as np
from jax import lax

PIX = 128
PW = 16
RY = 2
RX = 2
K_MAX = 13
ITERS = 2
P_SIZE = 16
NPH = 64


def draw_offsets(key, part):
    span_all = (2 * RY + 1) * (2 * RX + 1)
    center_code = RY * (2 * RX + 1) + RX
    row_keys = jax.random.split(key, P_SIZE)

    def one_row(row_key):
        order = jax.random.permutation(row_key, span_all - 1).astype(jnp.int32)
        picked = order[:K_MAX - 1]
        picked = picked + (picked >= center_code).astype(jnp.int32)
        return jnp.concatenate([jnp.full((1,), center_code, jnp.int32), picked])
    return jax.vmap(one_row)(row_keys)


def draw_volume_init(key, part):
    full_shape = (P_SIZE, NPH, PW, PIX)
    lateral_shape = (NPH, PW, PIX)
    back_lo, back_hi, bright_share, bright_lo, bright_hi, gain_lo, gain_hi = (0.3, 1.0, 0.08, 2.0, 6.0, 0.5, 1.5)
    background = jax.random.uniform(jax.random.fold_in(key, 21), full_shape, jnp.float32, back_lo, back_hi)
    bright_mask = jax.random.uniform(jax.random.fold_in(key, 22), lateral_shape, jnp.float32) < bright_share
    bright_vals = jax.random.uniform(jax.random.fold_in(key, 23), lateral_shape, jnp.float32, bright_lo, bright_hi)
    common = jnp.where(bright_mask, bright_vals, jnp.zeros_like(bright_vals))
    depth_gain = jax.random.uniform(jax.random.fold_in(key, 24), full_shape, jnp.float32, gain_lo, gain_hi)
    return (background + common[None] * depth_gain).astype(jnp.float32)


def draw_psf(key, part):
    full_shape = (P_SIZE, K_MAX, PIX, PIX)
    band_lo, band_hi, tail_lo, tail_hi = (0.5, 1.5, 0.01, 0.3)
    center_lo, center_hi, other_lo, other_hi = (4.0, 4.0, 0.3, 3.0)
    band_vals = jax.random.uniform(jax.random.fold_in(key, 31), full_shape, jnp.float32, band_lo, band_hi)
    tail_log = jax.random.uniform(jax.random.fold_in(key, 32), full_shape, jnp.float32, math.log(tail_lo), math.log(tail_hi))
    tail_part = 37.0 / PIX * jnp.exp(tail_log)
    shifts = jax.random.randint(jax.random.fold_in(key, 33), (P_SIZE, K_MAX), -(PIX // 8), PIX // 8 + 1).astype(jnp.int32)
    slot_ids = jnp.arange(K_MAX, dtype=jnp.int32)
    shifts = jnp.where(slot_ids[None, :] == 0, jnp.zeros_like(shifts), shifts)
    pixel_rows = jnp.arange(PIX, dtype=jnp.int32)[:, None]
    pixel_cols = jnp.arange(PIX, dtype=jnp.int32)[None, :]
    band_dist = jnp.mod(pixel_rows[None, None] - pixel_cols[None, None] - shifts[:, :, None, None], PIX)
    in_band = (band_dist <= 3) | (band_dist >= PIX - 3)
    block_vals = jnp.where(in_band, band_vals, tail_part)
    center_scale = jax.random.uniform(jax.random.fold_in(key, 34), (P_SIZE, 1), jnp.float32, center_lo, center_hi)
    other_log = jax.random.uniform(jax.random.fold_in(key, 35), (P_SIZE, K_MAX - 1), jnp.float32, math.log(other_lo), math.log(other_hi))
    scales = jnp.concatenate([center_scale, jnp.exp(other_log)], axis=1)
    result = block_vals * scales[:, :, None, None] / (10.0 * P_SIZE * K_MAX)
    return result.astype(jnp.bfloat16)


def levels(stream_key, extent, shards, smallest, top_value):
    factor_of, own = 1.0, jax.random.fold_in(stream_key, 6)
    for dim, shards_of in shards:
        steps = jnp.exp(jax.random.uniform(jax.random.fold_in(own, dim), (shards_of,), jnp.float32, smallest / len(shards), top_value / len(shards)))
        factor_of = factor_of * jnp.repeat(steps, extent[dim] // shards_of).reshape([-1 if axis == dim else 1 for axis in range(len(extent))])
    return factor_of


def split_up(amount, total, most, lean):
    weights = [(1 << 20) // math.isqrt(standing ** lean) + 1 for standing in range(2, amount + 1)]
    rest, given = total - most - (amount - 1), [1] * (amount - 1)
    while rest > 0:
        free = [i for i in range(amount - 1) if given[i] < most]
        mass, left = sum([weights[i] for i in free]), rest
        for i in free:
            more = min(most - given[i], max(1, left * weights[i] // mass), rest)
            given[i] = given[i] + more
            rest = rest - more
    return np.array([most] + given)


def ragged_sizes(stream_key, amount, total, bound, lean):
    if amount == 2:
        one = jax.random.randint(stream_key, (), max(1, total - bound), min(bound, total - 1) + 1)
        return jnp.stack([one, total - one])
    lengths = jnp.asarray(split_up(amount, total, bound, lean), jnp.int32)
    pairs = (amount - 1) // 2
    donor, sink = lengths[1:1 + 2 * pairs:2], lengths[2:2 + 2 * pairs:2]
    margin = jnp.minimum(donor - 1, bound - sink)
    shifted = jax.random.randint(jax.random.fold_in(stream_key, 1), (pairs,), 0, 1 << 20) % (margin + 1)
    lengths = lengths.at[1:1 + 2 * pairs:2].set(donor - shifted).at[2:2 + 2 * pairs:2].set(sink + shifted)
    return lengths[jax.random.permutation(jax.random.fold_in(stream_key, 2), amount)]


def setup_inputs(seed: int = 0) -> dict:
    streams_of = jax.random.split(jax.random.key(seed), 6)
    return {
        "volume_init": draw_volume_init(jax.random.fold_in(streams_of[5], 71), 0),
        "measured": jnp.clip(jnp.exp(math.log(4.0) - 2.7725887 * jax.random.uniform(streams_of[1], (NPH, PW, PIX), jnp.float32) ** levels(streams_of[1], (NPH, PW, PIX), ((0, 8),), -0.2, 0.2)), 0.25, 4.0),
        "psf": draw_psf(jax.random.fold_in(streams_of[5], 71), 0),
        "offsets": draw_offsets(jax.random.fold_in(streams_of[5], 71), 0),
        "counts": ragged_sizes(streams_of[4], P_SIZE, P_SIZE * K_MAX * 5 // 8, K_MAX, 2).astype(jnp.int32),
    }


def decode_offsets(offsets):
    span_x = 2 * RX + 1
    return (offsets // span_x - RY).astype(jnp.int32), (offsets % span_x - RX).astype(jnp.int32)


def keep_live(psf, counts):
    slot_ids = jnp.arange(K_MAX, dtype=jnp.int32)
    live = slot_ids[None, :] < counts[:, None]
    return jnp.where(live[:, :, None, None], psf, jnp.zeros_like(psf))


def rounded(field):
    return lax.optimization_barrier(field.astype(jnp.bfloat16)).astype(jnp.float32)


def reference(volume_init, measured, psf, offsets, counts):
    weights = keep_live(psf, counts).astype(jnp.float32)
    shift_rows, shift_cols = decode_offsets(offsets)
    zero_index = jnp.zeros((), jnp.int32)
    row_ids = jnp.arange(NPH, dtype=jnp.int32)
    col_ids = jnp.arange(PW, dtype=jnp.int32)
    volume = volume_init
    for repeat in range(ITERS):
        padded = jnp.pad(rounded(volume), ((0, 0), (RY, RY), (RX, RX), (0, 0)))

        def add_depth(sensor, item):
            plane, blocks, rows_by, cols_by = item

            def add_slot(slot_id, running):
                window = lax.dynamic_slice(plane, ((RY + rows_by[slot_id]).astype(jnp.int32), (RX + cols_by[slot_id]).astype(jnp.int32), zero_index), (NPH, PW, PIX))
                product = jnp.dot(window.reshape(NPH * PW, PIX), blocks[slot_id], precision=lax.Precision.HIGHEST)
                return running + product.reshape(NPH, PW, PIX)

            return lax.fori_loop(0, K_MAX, add_slot, sensor), None

        sensor = lax.scan(add_depth, jnp.zeros((NPH, PW, PIX), jnp.float32), (padded, weights, shift_rows, shift_cols))[0]
        ratio_pad = jnp.pad(rounded(measured / sensor), ((RY, RY), (RX, RX), (0, 0)))

        def update_depth(item):
            plane, blocks, rows_by, cols_by = item

            def add_slot(slot_id, running):
                window = lax.dynamic_slice(ratio_pad, ((RY - rows_by[slot_id]).astype(jnp.int32), (RX - cols_by[slot_id]).astype(jnp.int32), zero_index), (NPH, PW, PIX))
                product = jnp.dot(window.reshape(NPH * PW, PIX), blocks[slot_id].T, precision=lax.Precision.HIGHEST)
                return running + product.reshape(NPH, PW, PIX)

            back = lax.fori_loop(0, K_MAX, add_slot, jnp.zeros((NPH, PW, PIX), jnp.float32))
            source_rows = row_ids[None, :] - rows_by[:, None]
            source_cols = col_ids[None, :] - cols_by[:, None]
            inside_rows = (source_rows >= 0) & (source_rows < NPH)
            inside_cols = (source_cols >= 0) & (source_cols < PW)
            inside = (inside_rows[:, :, None] & inside_cols[:, None, :]).astype(jnp.float32)
            column_sums = jnp.sum(blocks, axis=2)
            coverage = jnp.einsum("kyx,kj->yxj", inside, column_sums, precision=lax.Precision.HIGHEST)
            return plane * back / coverage

        volume = lax.map(update_depth, (volume, weights, shift_rows, shift_cols))
    return volume
```

```python
import functools

import jax
import jax.numpy as jnp
from jax import lax
from jax.experimental import pallas as pl
from jax.experimental.pallas import tpu as pltpu
from jax.sharding import PartitionSpec as P

RY = 2
RX = 2
SX = 2 * RX + 1
ITERS = 2
MESH = pl.DeviceIdType.MESH


def kernel(
    D, L, planes, slots, rows, cols,
    at_ref, vol_hbm, meas_hbm, psf_hbm, out_ref,
    w, vol, meas, cov, xs, rs, cs, part, recv_own, recv_halo, rchunk, rext, total,
    load_sem, s_own, r_own, s_halo, r_halo, s_rat, s_rath, r_rat,
):
    d = lax.axis_index("depth")
    b = lax.axis_index("lat")
    pix = 128
    own = rows * cols
    chunk = own // D
    halo = RY * cols
    h = halo // chunk
    ext = own + 2 * halo
    out_rows = rows + 2 * RY
    f_zero = rows + 2 * RY
    f_rows = f_zero + out_rows
    b_rows = rows + 2 * RY + rows
    b_zero = rows + 2 * RY
    up = lax.rem(b + L - 1, L)
    down = lax.rem(b + 1, L)
    has_up = b > 0
    has_down = b < L - 1
    first = d < h
    last = d >= D - h

    loads = [pltpu.make_async_copy(vol_hbm, vol, load_sem.at[planes])]
    for p in range(planes):
        loads.append(
            pltpu.make_async_copy(
                psf_hbm.at[p], w.at[pl.ds(p * slots, slots)], load_sem.at[p]
            )
        )
    loads.append(
        pltpu.make_async_copy(
            meas_hbm.at[pl.ds(pl.multiple_of(d * chunk, chunk), chunk)],
            meas,
            load_sem.at[planes + 1],
        )
    )
    for copy in loads:
        copy.start()

    barrier = pltpu.get_barrier_semaphore()

    def greet(to_d, to_b):
        pl.semaphore_signal(barrier, inc=1, device_id=(to_d, to_b), device_id_type=MESH)

    for t in range(1, D):
        greet(lax.rem(d + t, D), b)

    @pl.when(has_up)
    def _():
        for c in range(D - h, D):
            greet(c, up)

    @pl.when(has_up & first)
    def _():
        for c in range(D - h):
            greet(c, up)

    @pl.when(has_down)
    def _():
        for c in range(h):
            greet(c, down)

    @pl.when(has_down & last)
    def _():
        for c in range(h, D):
            greet(c, down)

    fwd_at = [at_ref[0, d * planes + p, k] for p in range(planes) for k in range(slots)]
    back_at = [at_ref[1, d * planes + p, k] for p in range(planes) for k in range(slots)]

    def zeros(count):
        return jnp.zeros((count, cols, pix), jnp.bfloat16)

    for p in range(planes):
        for s in range(SX):
            xs[p, pl.ds(s * f_rows, 2 * RY)] = zeros(2 * RY)
            xs[p, pl.ds(s * f_rows + 2 * RY + rows, f_rows - 2 * RY - rows)] = zeros(
                f_rows - 2 * RY - rows
            )
    for s in range(SX):
        rs[pl.ds(s * b_rows + b_zero, rows)] = zeros(rows)
        cs[pl.ds(s * b_rows + b_zero, rows)] = zeros(rows)

    def shifted(flat, s):
        count = flat.shape[0]
        move = s - RX
        if move:
            col = lax.broadcasted_iota(jnp.int32, (count, pix), 0) % cols + move
            flat = pltpu.roll(flat, (-move) % count, 0)
            flat = jnp.where((col >= 0) & (col < cols), flat, 0.0)
        return flat.astype(jnp.bfloat16).reshape(count // cols, cols, pix)

    def spread_plane(p, plane):
        for s in range(SX):
            xs[p, pl.ds(s * f_rows + 2 * RY, rows)] = shifted(plane, s)

    def spread_ratio(ref, flat):
        for s in range(SX):
            ref[pl.ds(s * b_rows, out_rows)] = shifted(flat, s)

    def forward():
        acc = jnp.zeros((ext, pix), jnp.float32)
        q = 0
        while q < planes * slots:
            step = min(2, planes * slots - q)
            wins = [
                xs[i // slots, pl.ds(fwd_at[i], out_rows)].reshape(ext, pix)
                for i in range(q, q + step)
            ]
            lhs = jnp.concatenate(wins, axis=1) if step > 1 else wins[0]
            rhs = w[pl.ds(q, step)].reshape(step * pix, pix)
            acc = acc + jnp.dot(lhs, rhs, preferred_element_type=jnp.float32)
            q += step
        return acc

    def backward(ref, p):
        acc = jnp.zeros((own, pix), jnp.float32)
        k = 0
        while k < slots:
            step = min(2, slots - k)
            ids = [p * slots + i for i in range(k, k + step)]
            wins = [ref[pl.ds(back_at[i], rows)].reshape(own, pix) for i in ids]
            mats = [w[i] for i in ids]
            lhs = jnp.concatenate(wins, axis=1) if step > 1 else wins[0]
            rhs = jnp.concatenate(mats, axis=1) if step > 1 else mats[0]
            acc = acc + lax.dot_general(
                lhs, rhs, (((1,), (1,)), ((), ())), preferred_element_type=jnp.float32
            )
            k += step
        return acc

    def remote(src, dst, send, recv, to_d, to_b):
        return pltpu.make_async_remote_copy(
            src_ref=src,
            dst_ref=dst,
            send_sem=send,
            recv_sem=recv,
            device_id=(to_d, to_b),
            device_id_type=MESH,
        )

    def own_copy(it, t):
        c = lax.rem(d + t, D)
        return remote(
            part.at[it, h + c], recv_own.at[it, d], s_own.at[it, t], r_own.at[it, d], c, b
        )

    def own_arrival(it, t):
        c = lax.rem(d + t, D)
        return remote(
            part.at[it, h + c], recv_own.at[it, c], s_own.at[it, t], r_own.at[it, c], c, b
        )

    def up_copy(it, t):
        return remote(
            part.at[it, t], recv_halo.at[it, d], s_halo.at[it, t], r_halo.at[it, d],
            D - h + t, up,
        )

    def down_copy(it, t):
        return remote(
            part.at[it, h + D + t], recv_halo.at[it, d], s_halo.at[it, h + t],
            r_halo.at[it, d], t, down,
        )

    def halo_arrival(it, c, to_b):
        return remote(
            part.at[it, 0], recv_halo.at[it, c], s_halo.at[it, 0], r_halo.at[it, c], c, to_b
        )

    def ratio_copy(it, t):
        c = lax.rem(d + t, D)
        return remote(
            rchunk.at[it], rext.at[it, h + d], s_rat.at[it, t], r_rat.at[it, h + d], c, b
        )

    def ratio_arrival(it, slot, to_d, to_b):
        return remote(
            rchunk.at[it], rext.at[it, slot], s_rat.at[it, 0], r_rat.at[it, slot], to_d, to_b
        )

    def ratio_up(it, c):
        slot = h + D + lax.rem(d, h)
        return remote(
            rchunk.at[it], rext.at[it, slot], s_rath.at[it, c], r_rat.at[it, slot], c, up
        )

    def ratio_down(it, c):
        slot = lax.rem(d + h, D)
        return remote(
            rchunk.at[it], rext.at[it, slot], s_rath.at[it, c], r_rat.at[it, slot], c, down
        )

    ext_row = lax.broadcasted_iota(jnp.int32, (ext, pix), 0)
    low = jnp.where(has_up, 0, halo)
    high = jnp.where(has_down, ext, halo + own)
    spread_ratio(cs, jnp.where((ext_row >= low) & (ext_row < high), 1.0, 0.0))

    loads[0].wait()
    for p in range(planes):
        spread_plane(p, vol[p])

    for copy in loads[1:]:
        copy.wait()

    for it in range(ITERS):
        part[it] = forward().reshape(D + 2 * h, chunk, pix)
        if it == 0:
            amount = (
                (D - 1)
                + jnp.where(has_up, jnp.where(first, D, h), 0)
                + jnp.where(has_down, jnp.where(last, D, h), 0)
            )
            pl.semaphore_wait(barrier, amount)

        @pl.when(has_up)
        def _():
            for t in range(h):
                up_copy(it, t).start()

        @pl.when(has_down)
        def _():
            for t in range(h):
                down_copy(it, t).start()

        for t in range(1, D):
            own_copy(it, t).start()

        if it == 0:
            for p in range(planes):
                cov[p] = backward(cs, p)

        sensor = part[it, h + d]
        for t in range(1, D):
            own_arrival(it, t).wait_recv()
            sensor = sensor + recv_own[it, lax.rem(d + t, D)]

        @pl.when(has_up & first)
        def _():
            for c in range(D):
                halo_arrival(it, c, up).wait_recv()

        @pl.when(has_down & last)
        def _():
            for c in range(D):
                halo_arrival(it, c, down).wait_recv()

        total[...] = sensor

        @pl.when((has_up & first) | (has_down & last))
        def _():
            more = recv_halo[it, 0]
            for c in range(1, D):
                more = more + recv_halo[it, c]
            total[...] += more

        ratio = (meas[...] / total[...]).astype(jnp.bfloat16)
        rchunk[it] = ratio
        rext[it, h + d] = ratio

        @pl.when(has_up & first)
        def _():
            for c in range(D):
                ratio_up(it, c).start()

        @pl.when(has_down & last)
        def _():
            for c in range(D):
                ratio_down(it, c).start()

        for t in range(1, D):
            ratio_copy(it, t).start()

        @pl.when(has_up)
        def _():
            for t in range(h):
                ratio_arrival(it, t, D - h + t, up).wait_recv()

        @pl.when(jnp.logical_not(has_up))
        def _():
            for t in range(h):
                rext[it, t] = jnp.zeros((chunk, pix), jnp.bfloat16)

        @pl.when(has_down)
        def _():
            for t in range(h):
                ratio_arrival(it, h + D + t, t, down).wait_recv()

        @pl.when(jnp.logical_not(has_down))
        def _():
            for t in range(h):
                rext[it, h + D + t] = jnp.zeros((chunk, pix), jnp.bfloat16)

        for t in range(1, D):
            c = lax.rem(d + t, D)
            ratio_arrival(it, h + c, c, b).wait_recv()

        spread_ratio(rs, rext[it].astype(jnp.float32).reshape(ext, pix))
        for p in range(planes):
            plane = vol[p] * backward(rs, p) / cov[p]
            if it < ITERS - 1:
                vol[p] = plane
                spread_plane(p, plane)
            else:
                out_ref[p] = plane

    for it in range(ITERS):
        for t in range(1, D):
            own_copy(it, t).wait_send()
            ratio_copy(it, t).wait_send()

        @pl.when(has_up)
        def _():
            for t in range(h):
                up_copy(it, t).wait_send()

        @pl.when(has_down)
        def _():
            for t in range(h):
                down_copy(it, t).wait_send()

        @pl.when(has_up & first)
        def _():
            for c in range(D):
                ratio_up(it, c).wait_send()

        @pl.when(has_down & last)
        def _():
            for c in range(D):
                ratio_down(it, c).wait_send()


def shards(D, L, volume_init, measured, psf, offsets, counts):
    planes, rows, cols, pix = volume_init.shape
    slots = psf.shape[1]
    own = rows * cols
    chunk = own // D
    h = RY * cols // chunk
    f_rows = 2 * (rows + 2 * RY)
    b_rows = 2 * rows + 2 * RY
    row = offsets // SX
    col = offsets % SX
    alive = jnp.arange(slots, dtype=jnp.int32)[None, :] < counts[:, None]
    zero_at = rows + 2 * RY
    table = jnp.stack(
        [
            jnp.where(alive, col * f_rows + row, zero_at),
            jnp.where(alive, (SX - 1 - col) * b_rows + (2 * RY - row), zero_at),
        ]
    )
    dma = pltpu.SemaphoreType.DMA
    out = pl.pallas_call(
        functools.partial(kernel, D, L, planes, slots, rows, cols),
        out_shape=jax.ShapeDtypeStruct((planes, own, pix), jnp.float32),
        in_specs=[pl.BlockSpec(memory_space=pltpu.SMEM)]
        + [pl.BlockSpec(memory_space=pl.ANY)] * 3,
        out_specs=pl.BlockSpec(memory_space=pltpu.VMEM),
        scratch_shapes=[
            pltpu.VMEM((planes * slots, pix, pix), jnp.bfloat16),
            pltpu.VMEM((planes, own, pix), jnp.float32),
            pltpu.VMEM((chunk, pix), jnp.float32),
            pltpu.VMEM((planes, own, pix), jnp.float32),
            pltpu.VMEM((planes, SX * f_rows, cols, pix), jnp.bfloat16),
            pltpu.VMEM((SX * b_rows, cols, pix), jnp.bfloat16),
            pltpu.VMEM((SX * b_rows, cols, pix), jnp.bfloat16),
            pltpu.VMEM((ITERS, D + 2 * h, chunk, pix), jnp.float32),
            pltpu.VMEM((ITERS, D, chunk, pix), jnp.float32),
            pltpu.VMEM((ITERS, D, chunk, pix), jnp.float32),
            pltpu.VMEM((ITERS, chunk, pix), jnp.bfloat16),
            pltpu.VMEM((ITERS, D + 2 * h, chunk, pix), jnp.bfloat16),
            pltpu.VMEM((chunk, pix), jnp.float32),
            dma((planes + 2,)),
            dma((ITERS, D)),
            dma((ITERS, D)),
            dma((ITERS, 2 * h)),
            dma((ITERS, D)),
            dma((ITERS, D)),
            dma((ITERS, D)),
            dma((ITERS, D + 2 * h)),
        ],
        compiler_params=pltpu.CompilerParams(
            collective_id=0, has_side_effects=True, vmem_limit_bytes=32 * 1024 * 1024
        ),
    )(
        table,
        volume_init.reshape(planes, own, pix),
        measured.reshape(own, pix),
        psf,
    )
    return out.reshape(planes, rows, cols, pix)


def solution(mesh):
    return jax.shard_map(
        functools.partial(shards, mesh.shape["depth"], mesh.shape["lat"]),
        mesh=mesh,
        in_specs=(
            P("depth", "lat", None, None),
            P("lat", None, None),
            P("depth", None, None, None),
            P(),
            P(),
        ),
        out_specs=P("depth", "lat", None, None),
        check_vma=False,
    )
```

```python
import functools

import jax
import jax.numpy as jnp
from jax import lax
from jax.experimental import pallas as pl
from jax.experimental.pallas import tpu as pltpu
from jax.sharding import PartitionSpec as P

RY = 2
RX = 2
SX = 2 * RX + 1
ITERS = 2
MESH = pl.DeviceIdType.MESH


def kernel(
    D, L, planes, slots, rows, cols,
    at_ref, vol_hbm, meas_hbm, psf_hbm, out_ref,
    w, vol, meas, cov, xs, rs, cs, part, recv_own, recv_halo, rchunk, rext, total,
    load_sem, s_own, r_own, s_halo, r_halo, s_rat, s_rath, r_rat,
):
    d = lax.axis_index("depth")
    b = lax.axis_index("lat")
    pix = 128
    own = rows * cols
    chunk = own // D
    halo = RY * cols
    h = halo // chunk
    ext = own + 2 * halo
    out_rows = rows + 2 * RY
    f_zero = rows + 2 * RY
    f_rows = f_zero + out_rows
    b_rows = rows + 2 * RY + rows
    b_zero = rows + 2 * RY
    up = lax.rem(b + L - 1, L)
    down = lax.rem(b + 1, L)
    has_up = b > 0
    has_down = b < L - 1
    first = d < h
    last = d >= D - h

    loads = [pltpu.make_async_copy(vol_hbm, vol, load_sem.at[planes])]
    for p in range(planes):
        loads.append(
            pltpu.make_async_copy(
                psf_hbm.at[p], w.at[pl.ds(p * slots, slots)], load_sem.at[p]
            )
        )
    loads.append(
        pltpu.make_async_copy(
            meas_hbm.at[pl.ds(pl.multiple_of(d * chunk, chunk), chunk)],
            meas,
            load_sem.at[planes + 1],
        )
    )
    for copy in loads:
        copy.start()

    barrier = pltpu.get_barrier_semaphore()

    def greet(to_d, to_b):
        pl.semaphore_signal(barrier, inc=1, device_id=(to_d, to_b), device_id_type=MESH)

    for t in range(1, D):
        greet(lax.rem(d + t, D), b)

    @pl.when(has_up)
    def _():
        for c in range(D - h, D):
            greet(c, up)

    @pl.when(has_up & first)
    def _():
        for c in range(D - h):
            greet(c, up)

    @pl.when(has_down)
    def _():
        for c in range(h):
            greet(c, down)

    @pl.when(has_down & last)
    def _():
        for c in range(h, D):
            greet(c, down)

    fwd_at = [at_ref[0, d * planes + p, k] for p in range(planes) for k in range(slots)]
    back_at = [at_ref[1, d * planes + p, k] for p in range(planes) for k in range(slots)]

    def zeros(count):
        return jnp.zeros((count, cols, pix), jnp.bfloat16)

    for p in range(planes):
        for s in range(SX):
            xs[p, pl.ds(s * f_rows, 2 * RY)] = zeros(2 * RY)
            xs[p, pl.ds(s * f_rows + 2 * RY + rows, f_rows - 2 * RY - rows)] = zeros(
                f_rows - 2 * RY - rows
            )
    for s in range(SX):
        rs[pl.ds(s * b_rows + b_zero, rows)] = zeros(rows)
        cs[pl.ds(s * b_rows + b_zero, rows)] = zeros(rows)

    def shifted(flat, s):
        count = flat.shape[0]
        move = s - RX
        if move:
            col = lax.broadcasted_iota(jnp.int32, (count, pix), 0) % cols + move
            flat = pltpu.roll(flat, (-move) % count, 0)
            flat = jnp.where((col >= 0) & (col < cols), flat, 0.0)
        return flat.astype(jnp.bfloat16).reshape(count // cols, cols, pix)

    def spread_plane(p, plane):
        for s in range(SX):
            xs[p, pl.ds(s * f_rows + 2 * RY, rows)] = shifted(plane, s)

    def spread_ratio(ref, flat):
        for s in range(SX):
            ref[pl.ds(s * b_rows, out_rows)] = shifted(flat, s)

    def forward():
        acc = jnp.zeros((ext, pix), jnp.float32)
        q = 0
        while q < planes * slots:
            step = min(2, planes * slots - q)
            wins = [
                xs[i // slots, pl.ds(fwd_at[i], out_rows)].reshape(ext, pix)
                for i in range(q, q + step)
            ]
            lhs = jnp.concatenate(wins, axis=1) if step > 1 else wins[0]
            rhs = w[pl.ds(q, step)].reshape(step * pix, pix)
            acc = acc + jnp.dot(lhs, rhs, preferred_element_type=jnp.float32)
            q += step
        return acc

    def backward(ref, p):
        acc = jnp.zeros((own, pix), jnp.float32)
        k = 0
        while k < slots:
            step = min(2, slots - k)
            ids = [p * slots + i for i in range(k, k + step)]
            wins = [ref[pl.ds(back_at[i], rows)].reshape(own, pix) for i in ids]
            mats = [w[i] for i in ids]
            lhs = jnp.concatenate(wins, axis=1) if step > 1 else wins[0]
            rhs = jnp.concatenate(mats, axis=1) if step > 1 else mats[0]
            acc = acc + lax.dot_general(
                lhs, rhs, (((1,), (1,)), ((), ())), preferred_element_type=jnp.float32
            )
            k += step
        return acc

    def remote(src, dst, send, recv, to_d, to_b):
        return pltpu.make_async_remote_copy(
            src_ref=src,
            dst_ref=dst,
            send_sem=send,
            recv_sem=recv,
            device_id=(to_d, to_b),
            device_id_type=MESH,
        )

    def own_copy(it, t):
        c = lax.rem(d + t, D)
        return remote(
            part.at[it, h + c], recv_own.at[it, d], s_own.at[it, t], r_own.at[it, d], c, b
        )

    def own_arrival(it, t):
        c = lax.rem(d + t, D)
        return remote(
            part.at[it, h + c], recv_own.at[it, c], s_own.at[it, t], r_own.at[it, c], c, b
        )

    def up_copy(it, t):
        return remote(
            part.at[it, t], recv_halo.at[it, d], s_halo.at[it, t], r_halo.at[it, d],
            D - h + t, up,
        )

    def down_copy(it, t):
        return remote(
            part.at[it, h + D + t], recv_halo.at[it, d], s_halo.at[it, h + t],
            r_halo.at[it, d], t, down,
        )

    def halo_arrival(it, c, to_b):
        return remote(
            part.at[it, 0], recv_halo.at[it, c], s_halo.at[it, 0], r_halo.at[it, c], c, to_b
        )

    def ratio_copy(it, t):
        c = lax.rem(d + t, D)
        return remote(
            rchunk.at[it], rext.at[it, h + d], s_rat.at[it, t], r_rat.at[it, h + d], c, b
        )

    def ratio_arrival(it, slot, to_d, to_b):
        return remote(
            rchunk.at[it], rext.at[it, slot], s_rat.at[it, 0], r_rat.at[it, slot], to_d, to_b
        )

    def ratio_up(it, c):
        slot = h + D + lax.rem(d, h)
        return remote(
            rchunk.at[it], rext.at[it, slot], s_rath.at[it, c], r_rat.at[it, slot], c, up
        )

    def ratio_down(it, c):
        slot = lax.rem(d + h, D)
        return remote(
            rchunk.at[it], rext.at[it, slot], s_rath.at[it, c], r_rat.at[it, slot], c, down
        )

    ext_row = lax.broadcasted_iota(jnp.int32, (ext, pix), 0)
    low = jnp.where(has_up, 0, halo)
    high = jnp.where(has_down, ext, halo + own)
    spread_ratio(cs, jnp.where((ext_row >= low) & (ext_row < high), 1.0, 0.0))

    loads[0].wait()
    for p in range(planes):
        spread_plane(p, vol[p])

    for copy in loads[1:]:
        copy.wait()

    early = planes // 2

    for it in range(ITERS):
        part[it] = forward().reshape(D + 2 * h, chunk, pix)
        if it == 0:
            amount = (
                (D - 1)
                + jnp.where(has_up, jnp.where(first, D, h), 0)
                + jnp.where(has_down, jnp.where(last, D, h), 0)
            )
            pl.semaphore_wait(barrier, amount)

        @pl.when(has_up)
        def _():
            for t in range(h):
                up_copy(it, t).start()

        @pl.when(has_down)
        def _():
            for t in range(h):
                down_copy(it, t).start()

        for t in range(1, D):
            own_copy(it, t).start()

        if it == 0:
            for p in range(early):
                cov[p] = backward(cs, p)

        sensor = part[it, h + d]
        for t in range(1, D):
            own_arrival(it, t).wait_recv()
            sensor = sensor + recv_own[it, lax.rem(d + t, D)]

        @pl.when(has_up & first)
        def _():
            for c in range(D):
                halo_arrival(it, c, up).wait_recv()

        @pl.when(has_down & last)
        def _():
            for c in range(D):
                halo_arrival(it, c, down).wait_recv()

        total[...] = sensor

        @pl.when((has_up & first) | (has_down & last))
        def _():
            more = recv_halo[it, 0]
            for c in range(1, D):
                more = more + recv_halo[it, c]
            total[...] += more

        ratio = (meas[...] / total[...]).astype(jnp.bfloat16)
        rchunk[it] = ratio
        rext[it, h + d] = ratio

        @pl.when(has_up & first)
        def _():
            for c in range(D):
                ratio_up(it, c).start()

        @pl.when(has_down & last)
        def _():
            for c in range(D):
                ratio_down(it, c).start()

        for t in range(1, D):
            ratio_copy(it, t).start()

        if it == 0:
            for p in range(early, planes):
                cov[p] = backward(cs, p)

        @pl.when(has_up)
        def _():
            for t in range(h):
                ratio_arrival(it, t, D - h + t, up).wait_recv()

        @pl.when(jnp.logical_not(has_up))
        def _():
            for t in range(h):
                rext[it, t] = jnp.zeros((chunk, pix), jnp.bfloat16)

        @pl.when(has_down)
        def _():
            for t in range(h):
                ratio_arrival(it, h + D + t, t, down).wait_recv()

        @pl.when(jnp.logical_not(has_down))
        def _():
            for t in range(h):
                rext[it, h + D + t] = jnp.zeros((chunk, pix), jnp.bfloat16)

        for t in range(1, D):
            c = lax.rem(d + t, D)
            ratio_arrival(it, h + c, c, b).wait_recv()

        spread_ratio(rs, rext[it].astype(jnp.float32).reshape(ext, pix))
        for p in range(planes):
            plane = vol[p] * backward(rs, p) / cov[p]
            if it < ITERS - 1:
                vol[p] = plane
                spread_plane(p, plane)
            else:
                out_ref[p] = plane

    for it in range(ITERS):
        for t in range(1, D):
            own_copy(it, t).wait_send()
            ratio_copy(it, t).wait_send()

        @pl.when(has_up)
        def _():
            for t in range(h):
                up_copy(it, t).wait_send()

        @pl.when(has_down)
        def _():
            for t in range(h):
                down_copy(it, t).wait_send()

        @pl.when(has_up & first)
        def _():
            for c in range(D):
                ratio_up(it, c).wait_send()

        @pl.when(has_down & last)
        def _():
            for c in range(D):
                ratio_down(it, c).wait_send()


def shards(D, L, volume_init, measured, psf, offsets, counts):
    planes, rows, cols, pix = volume_init.shape
    slots = psf.shape[1]
    own = rows * cols
    chunk = own // D
    h = RY * cols // chunk
    f_rows = 2 * (rows + 2 * RY)
    b_rows = 2 * rows + 2 * RY
    row = offsets // SX
    col = offsets % SX
    alive = jnp.arange(slots, dtype=jnp.int32)[None, :] < counts[:, None]
    zero_at = rows + 2 * RY
    table = jnp.stack(
        [
            jnp.where(alive, col * f_rows + row, zero_at),
            jnp.where(alive, (SX - 1 - col) * b_rows + (2 * RY - row), zero_at),
        ]
    )
    in_hbm = functools.partial(pltpu.with_memory_space_constraint, memory_space=pltpu.HBM)
    dma = pltpu.SemaphoreType.DMA
    out = pl.pallas_call(
        functools.partial(kernel, D, L, planes, slots, rows, cols),
        out_shape=jax.ShapeDtypeStruct((planes, own, pix), jnp.float32),
        in_specs=[pl.BlockSpec(memory_space=pltpu.SMEM)]
        + [pl.BlockSpec(memory_space=pltpu.HBM)] * 3,
        out_specs=pl.BlockSpec(memory_space=pltpu.VMEM),
        scratch_shapes=[
            pltpu.VMEM((planes * slots, pix, pix), jnp.bfloat16),
            pltpu.VMEM((planes, own, pix), jnp.float32),
            pltpu.VMEM((chunk, pix), jnp.float32),
            pltpu.VMEM((planes, own, pix), jnp.float32),
            pltpu.VMEM((planes, SX * f_rows, cols, pix), jnp.bfloat16),
            pltpu.VMEM((SX * b_rows, cols, pix), jnp.bfloat16),
            pltpu.VMEM((SX * b_rows, cols, pix), jnp.bfloat16),
            pltpu.VMEM((ITERS, D + 2 * h, chunk, pix), jnp.float32),
            pltpu.VMEM((ITERS, D, chunk, pix), jnp.float32),
            pltpu.VMEM((ITERS, D, chunk, pix), jnp.float32),
            pltpu.VMEM((ITERS, chunk, pix), jnp.bfloat16),
            pltpu.VMEM((ITERS, D + 2 * h, chunk, pix), jnp.bfloat16),
            pltpu.VMEM((chunk, pix), jnp.float32),
            dma((planes + 2,)),
            dma((ITERS, D)),
            dma((ITERS, D)),
            dma((ITERS, 2 * h)),
            dma((ITERS, D)),
            dma((ITERS, D)),
            dma((ITERS, D)),
            dma((ITERS, D + 2 * h)),
        ],
        compiler_params=pltpu.CompilerParams(
            collective_id=0, has_side_effects=True, vmem_limit_bytes=32 * 1024 * 1024
        ),
    )(
        table,
        in_hbm(volume_init.reshape(planes, own, pix)),
        in_hbm(measured.reshape(own, pix)),
        in_hbm(psf),
    )
    return out.reshape(planes, rows, cols, pix)


def solution(mesh):
    return jax.shard_map(
        functools.partial(shards, mesh.shape["depth"], mesh.shape["lat"]),
        mesh=mesh,
        in_specs=(
            P("depth", "lat", None, None),
            P("lat", None, None),
            P("depth", None, None, None),
            P(),
            P(),
        ),
        out_specs=P("depth", "lat", None, None),
        check_vma=False,
    )
```

```python
import functools

import jax
import jax.numpy as jnp
from jax import lax
from jax.experimental import pallas as pl
from jax.experimental.pallas import tpu as pltpu
from jax.sharding import PartitionSpec as P

RY = 2
RX = 2
SX = 2 * RX + 1
ITERS = 2
MESH = pl.DeviceIdType.MESH


def kernel(
    D, L, planes, slots, rows, cols,
    at_ref, vol_hbm, meas_hbm, psf_hbm, out_ref,
    w, vol, meas, cov, xs, rs, cs, part, recv_own, recv_halo, rchunk, rext, total,
    load_sem, s_own, r_own, s_halo, r_halo, s_rat, s_rath, r_rat,
):
    d = lax.axis_index("depth")
    b = lax.axis_index("lat")
    pix = 128
    own = rows * cols
    chunk = own // D
    halo = RY * cols
    h = halo // chunk
    ext = own + 2 * halo
    out_rows = rows + 2 * RY
    f_zero = rows + 2 * RY
    f_rows = f_zero + out_rows
    b_rows = rows + 2 * RY + rows
    b_zero = rows + 2 * RY
    up = lax.rem(b + L - 1, L)
    down = lax.rem(b + 1, L)
    has_up = b > 0
    has_down = b < L - 1
    first = d < h
    last = d >= D - h

    loads = [pltpu.make_async_copy(vol_hbm, vol, load_sem.at[planes])]
    for p in range(planes):
        loads.append(
            pltpu.make_async_copy(
                psf_hbm.at[p], w.at[pl.ds(p * slots, slots)], load_sem.at[p]
            )
        )
    loads.append(
        pltpu.make_async_copy(
            meas_hbm.at[pl.ds(pl.multiple_of(d * chunk, chunk), chunk)],
            meas,
            load_sem.at[planes + 1],
        )
    )
    for copy in loads:
        copy.start()

    barrier = pltpu.get_barrier_semaphore()

    def greet(to_d, to_b):
        pl.semaphore_signal(barrier, inc=1, device_id=(to_d, to_b), device_id_type=MESH)

    for t in range(1, D):
        greet(lax.rem(d + t, D), b)

    @pl.when(has_up)
    def _():
        for c in range(D - h, D):
            greet(c, up)

    @pl.when(has_up & first)
    def _():
        for c in range(D - h):
            greet(c, up)

    @pl.when(has_down)
    def _():
        for c in range(h):
            greet(c, down)

    @pl.when(has_down & last)
    def _():
        for c in range(h, D):
            greet(c, down)

    fwd_at = [at_ref[0, d * planes + p, k] for p in range(planes) for k in range(slots)]
    back_at = [at_ref[1, d * planes + p, k] for p in range(planes) for k in range(slots)]

    def zeros(count):
        return jnp.zeros((count, cols, pix), jnp.bfloat16)

    for p in range(planes):
        for s in range(SX):
            xs[p, pl.ds(s * f_rows, 2 * RY)] = zeros(2 * RY)
            xs[p, pl.ds(s * f_rows + 2 * RY + rows, f_rows - 2 * RY - rows)] = zeros(
                f_rows - 2 * RY - rows
            )
    for s in range(SX):
        rs[pl.ds(s * b_rows + b_zero, rows)] = zeros(rows)
        cs[pl.ds(s * b_rows + b_zero, rows)] = zeros(rows)

    def shifted(flat, s):
        count = flat.shape[0]
        move = s - RX
        if move:
            col = lax.broadcasted_iota(jnp.int32, (count, pix), 0) % cols + move
            flat = pltpu.roll(flat, (-move) % count, 0)
            flat = jnp.where((col >= 0) & (col < cols), flat, 0.0)
        return flat.astype(jnp.bfloat16).reshape(count // cols, cols, pix)

    def spread_plane(p, plane):
        for s in range(SX):
            xs[p, pl.ds(s * f_rows + 2 * RY, rows)] = shifted(plane, s)

    def spread_ratio(ref, flat):
        for s in range(SX):
            ref[pl.ds(s * b_rows, out_rows)] = shifted(flat, s)

    def forward(arriving):
        landed = 0
        acc = jnp.zeros((ext, pix), jnp.float32)
        q = 0
        while q < planes * slots:
            step = min(4, planes * slots - q)
            while arriving and landed * slots < q + step:
                landed += 1
                loads[landed].wait()
            wins = [
                xs[i // slots, pl.ds(fwd_at[i], out_rows)].reshape(ext, pix)
                for i in range(q, q + step)
            ]
            lhs = jnp.concatenate(wins, axis=1) if step > 1 else wins[0]
            rhs = w[pl.ds(q, step)].reshape(step * pix, pix)
            acc = acc + jnp.dot(lhs, rhs, preferred_element_type=jnp.float32)
            q += step
        return acc

    def backward(ref, p):
        acc = jnp.zeros((own, pix), jnp.float32)
        k = 0
        while k < slots:
            step = min(4, slots - k)
            ids = [p * slots + i for i in range(k, k + step)]
            wins = [ref[pl.ds(back_at[i], rows)].reshape(own, pix) for i in ids]
            mats = [w[i] for i in ids]
            lhs = jnp.concatenate(wins, axis=1) if step > 1 else wins[0]
            rhs = jnp.concatenate(mats, axis=1) if step > 1 else mats[0]
            acc = acc + lax.dot_general(
                lhs, rhs, (((1,), (1,)), ((), ())), preferred_element_type=jnp.float32
            )
            k += step
        return acc

    def remote(src, dst, send, recv, to_d, to_b):
        return pltpu.make_async_remote_copy(
            src_ref=src,
            dst_ref=dst,
            send_sem=send,
            recv_sem=recv,
            device_id=(to_d, to_b),
            device_id_type=MESH,
        )

    def own_copy(it, t):
        c = lax.rem(d + t, D)
        return remote(
            part.at[it, h + c], recv_own.at[it, d], s_own.at[it, t], r_own.at[it, d], c, b
        )

    def own_arrival(it, t):
        c = lax.rem(d + t, D)
        return remote(
            part.at[it, h + c], recv_own.at[it, c], s_own.at[it, t], r_own.at[it, c], c, b
        )

    def up_copy(it, t):
        return remote(
            part.at[it, t], recv_halo.at[it, d], s_halo.at[it, t], r_halo.at[it, d],
            D - h + t, up,
        )

    def down_copy(it, t):
        return remote(
            part.at[it, h + D + t], recv_halo.at[it, d], s_halo.at[it, h + t],
            r_halo.at[it, d], t, down,
        )

    def halo_arrival(it, c, to_b):
        return remote(
            part.at[it, 0], recv_halo.at[it, c], s_halo.at[it, 0], r_halo.at[it, c], c, to_b
        )

    def ratio_copy(it, t):
        c = lax.rem(d + t, D)
        return remote(
            rchunk.at[it], rext.at[it, h + d], s_rat.at[it, t], r_rat.at[it, h + d], c, b
        )

    def ratio_arrival(it, slot, to_d, to_b):
        return remote(
            rchunk.at[it], rext.at[it, slot], s_rat.at[it, 0], r_rat.at[it, slot], to_d, to_b
        )

    def ratio_up(it, c):
        slot = h + D + lax.rem(d, h)
        return remote(
            rchunk.at[it], rext.at[it, slot], s_rath.at[it, c], r_rat.at[it, slot], c, up
        )

    def ratio_down(it, c):
        slot = lax.rem(d + h, D)
        return remote(
            rchunk.at[it], rext.at[it, slot], s_rath.at[it, c], r_rat.at[it, slot], c, down
        )

    ext_row = lax.broadcasted_iota(jnp.int32, (ext, pix), 0)
    low = jnp.where(has_up, 0, halo)
    high = jnp.where(has_down, ext, halo + own)
    spread_ratio(cs, jnp.where((ext_row >= low) & (ext_row < high), 1.0, 0.0))

    loads[0].wait()
    for p in range(planes):
        spread_plane(p, vol[p])

    early = planes // 2

    for it in range(ITERS):
        part[it] = forward(it == 0).reshape(D + 2 * h, chunk, pix)
        if it == 0:
            loads[planes + 1].wait()
            amount = (
                (D - 1)
                + jnp.where(has_up, jnp.where(first, D, h), 0)
                + jnp.where(has_down, jnp.where(last, D, h), 0)
            )
            pl.semaphore_wait(barrier, amount)

        @pl.when(has_up)
        def _():
            for t in range(h):
                up_copy(it, t).start()

        @pl.when(has_down)
        def _():
            for t in range(h):
                down_copy(it, t).start()

        for t in range(1, D):
            own_copy(it, t).start()

        if it == 0:
            for p in range(early):
                cov[p] = backward(cs, p)

        sensor = part[it, h + d]
        for t in range(1, D):
            own_arrival(it, t).wait_recv()
            sensor = sensor + recv_own[it, lax.rem(d + t, D)]

        @pl.when(has_up & first)
        def _():
            for c in range(D):
                halo_arrival(it, c, up).wait_recv()

        @pl.when(has_down & last)
        def _():
            for c in range(D):
                halo_arrival(it, c, down).wait_recv()

        total[...] = sensor

        @pl.when((has_up & first) | (has_down & last))
        def _():
            more = recv_halo[it, 0]
            for c in range(1, D):
                more = more + recv_halo[it, c]
            total[...] += more

        ratio = (meas[...] / total[...]).astype(jnp.bfloat16)
        rchunk[it] = ratio
        rext[it, h + d] = ratio

        @pl.when(has_up & first)
        def _():
            for c in range(D):
                ratio_up(it, c).start()

        @pl.when(has_down & last)
        def _():
            for c in range(D):
                ratio_down(it, c).start()

        for t in range(1, D):
            ratio_copy(it, t).start()

        if it == 0:
            for p in range(early, planes):
                cov[p] = backward(cs, p)

        @pl.when(has_up)
        def _():
            for t in range(h):
                ratio_arrival(it, t, D - h + t, up).wait_recv()

        @pl.when(jnp.logical_not(has_up))
        def _():
            for t in range(h):
                rext[it, t] = jnp.zeros((chunk, pix), jnp.bfloat16)

        @pl.when(has_down)
        def _():
            for t in range(h):
                ratio_arrival(it, h + D + t, t, down).wait_recv()

        @pl.when(jnp.logical_not(has_down))
        def _():
            for t in range(h):
                rext[it, h + D + t] = jnp.zeros((chunk, pix), jnp.bfloat16)

        for t in range(1, D):
            c = lax.rem(d + t, D)
            ratio_arrival(it, h + c, c, b).wait_recv()

        spread_ratio(rs, rext[it].astype(jnp.float32).reshape(ext, pix))
        for p in range(planes):
            plane = vol[p] * backward(rs, p) / cov[p]
            if it < ITERS - 1:
                vol[p] = plane
                spread_plane(p, plane)
            else:
                out_ref[p] = plane

    for it in range(ITERS):
        for t in range(1, D):
            own_copy(it, t).wait_send()
            ratio_copy(it, t).wait_send()

        @pl.when(has_up)
        def _():
            for t in range(h):
                up_copy(it, t).wait_send()

        @pl.when(has_down)
        def _():
            for t in range(h):
                down_copy(it, t).wait_send()

        @pl.when(has_up & first)
        def _():
            for c in range(D):
                ratio_up(it, c).wait_send()

        @pl.when(has_down & last)
        def _():
            for c in range(D):
                ratio_down(it, c).wait_send()


def shards(D, L, volume_init, measured, psf, offsets, counts):
    planes, rows, cols, pix = volume_init.shape
    slots = psf.shape[1]
    own = rows * cols
    chunk = own // D
    h = RY * cols // chunk
    f_rows = 2 * (rows + 2 * RY)
    b_rows = 2 * rows + 2 * RY
    row = offsets // SX
    col = offsets % SX
    alive = jnp.arange(slots, dtype=jnp.int32)[None, :] < counts[:, None]
    zero_at = rows + 2 * RY
    table = jnp.stack(
        [
            jnp.where(alive, col * f_rows + row, zero_at),
            jnp.where(alive, (SX - 1 - col) * b_rows + (2 * RY - row), zero_at),
        ]
    )
    in_hbm = functools.partial(pltpu.with_memory_space_constraint, memory_space=pltpu.HBM)
    dma = pltpu.SemaphoreType.DMA
    out = pl.pallas_call(
        functools.partial(kernel, D, L, planes, slots, rows, cols),
        out_shape=jax.ShapeDtypeStruct((planes, own, pix), jnp.float32),
        in_specs=[pl.BlockSpec(memory_space=pltpu.SMEM)]
        + [pl.BlockSpec(memory_space=pltpu.HBM)] * 3,
        out_specs=pl.BlockSpec(memory_space=pltpu.VMEM),
        scratch_shapes=[
            pltpu.VMEM((planes * slots, pix, pix), jnp.bfloat16),
            pltpu.VMEM((planes, own, pix), jnp.float32),
            pltpu.VMEM((chunk, pix), jnp.float32),
            pltpu.VMEM((planes, own, pix), jnp.float32),
            pltpu.VMEM((planes, SX * f_rows, cols, pix), jnp.bfloat16),
            pltpu.VMEM((SX * b_rows, cols, pix), jnp.bfloat16),
            pltpu.VMEM((SX * b_rows, cols, pix), jnp.bfloat16),
            pltpu.VMEM((ITERS, D + 2 * h, chunk, pix), jnp.float32),
            pltpu.VMEM((ITERS, D, chunk, pix), jnp.float32),
            pltpu.VMEM((ITERS, D, chunk, pix), jnp.float32),
            pltpu.VMEM((ITERS, chunk, pix), jnp.bfloat16),
            pltpu.VMEM((ITERS, D + 2 * h, chunk, pix), jnp.bfloat16),
            pltpu.VMEM((chunk, pix), jnp.float32),
            dma((planes + 2,)),
            dma((ITERS, D)),
            dma((ITERS, D)),
            dma((ITERS, 2 * h)),
            dma((ITERS, D)),
            dma((ITERS, D)),
            dma((ITERS, D)),
            dma((ITERS, D + 2 * h)),
        ],
        compiler_params=pltpu.CompilerParams(
            collective_id=0, has_side_effects=True, vmem_limit_bytes=32 * 1024 * 1024
        ),
    )(
        table,
        in_hbm(volume_init.reshape(planes, own, pix)),
        in_hbm(measured.reshape(own, pix)),
        in_hbm(psf),
    )
    return out.reshape(planes, rows, cols, pix)


def solution(mesh):
    return jax.shard_map(
        functools.partial(shards, mesh.shape["depth"], mesh.shape["lat"]),
        mesh=mesh,
        in_specs=(
            P("depth", "lat", None, None),
            P("lat", None, None),
            P("depth", None, None, None),
            P(),
            P(),
        ),
        out_specs=P("depth", "lat", None, None),
        check_vma=False,
    )
```
